32 devices in a mesh: dp: 2 (over y), row: 4 (over x, core), col: 4 (over z).
Axes of the slice: x: 2, y: 2, z: 4, core: 2. Of those that a mesh axis runs over, the one named last changes fastest.
Arguments:
- out_grad: float32 [128, 8192], P(('dp', 'row'), 'col'), parts along dimension 0, may hold values from -6 to 6
- hidden: float32 [128, 14336], P(('dp', 'col'), 'row'), parts along dimension 0, may hold values from -0.75 to 0.75
- weight: float32 [14336, 8192], P('row', 'col'), may hold values from -0.046875 to 0.046875
Outputs:
- weight_grad: float32 [28672, 8192], P(('dp', 'row'), 'col'), parts along dimension 0
- hidden_grad: float32 [128, 14336], P(('dp', 'col'), 'row'), parts along dimension 0
The draws below stay inside these ranges and needn't reach their ends.
There are 2 independent parts, one for each index of `dp`. The reference program is written for one: setup_inputs(seed, part) draws one part's arguments, and reference() takes and returns one part's arrays. A program takes and returns all parts, laid end to end along the dimension named above; an argument that names none is the same for every part. Nothing has to cross between parts.
All inputs are finite; a program needn't handle non-finite values.
Results may differ from the reference program's by a relative error of at most 0.000071.
Values sent between devices are 32-bit elements; how exact they have to be, the bound alone decides.
A program may use at most 128 MiB of HBM per device.

```python
import jax
import jax.numpy as jnp
from jax import lax

D = 8192
FF = 14336
TOKENS = 64


def spiked(drawn, rng, source, target, shards_of, factor):
    owner, partner = [(jnp.arange(drawn.shape[axis_at]) // (drawn.shape[axis_at] // shards_of)).reshape([-1 if axis == axis_at else 1 for axis in range(drawn.ndim)]) for axis_at in (source, target)]
    chosen = jax.random.permutation(rng, shards_of)[partner]
    strong = (owner == chosen) | (owner == (partner + shards_of // 2) % shards_of)
    return jnp.where(strong, factor * drawn, drawn)


def shard_levels(own_key, shape, pieces, low, high):
    factor_of, own = 1.0, jax.random.fold_in(own_key, 6)
    for position, parts in pieces:
        heights = jnp.exp(jax.random.uniform(jax.random.fold_in(own, position), (parts,), jnp.float32, low / len(pieces), high / len(pieces)))
        factor_of = factor_of * jnp.repeat(heights, shape[position] // parts).reshape([-1 if axis == position else 1 for axis in range(len(shape))])
    return factor_of


def gaussian(rng, extent, scale, bound, shards=(), dtype=jnp.bfloat16):
    gain = shard_levels(rng, extent, shards, -0.22, 0.18) if shards else 1.0
    result = jax.random.normal(rng, extent, jnp.float32) * scale * gain
    return jnp.minimum(jnp.maximum(result, -bound), bound).astype(dtype)


def gaussian_with(key, shape, scale, reach, shards, heavy, held_as=jnp.bfloat16):
    result = scale * jax.random.normal(key, shape, jnp.float32)
    if shards:
        result = result * shard_levels(key, shape, shards, -0.22, 0.18)
    return jnp.clip(spiked(result, jax.random.fold_in(key, 3), *heavy), -reach, reach).astype(held_as)


def setup_inputs(seed: int = 0, part: int = 0) -> dict:
    key_list = jax.random.split(jax.random.key(seed), 4)
    part_keys = jax.random.split(jax.random.fold_in(key_list[3], part), 4)
    out_grad = gaussian_with(part_keys[0], (TOKENS, D), 1.0, 6.0, ((0, 4), (1, 4)), (1, 0, 4, 2.0), jnp.float32)
    hidden = gaussian(part_keys[1], (TOKENS, FF), TOKENS ** -0.5, 0.75, ((0, 4), (1, 4)), jnp.float32)
    weight = gaussian(key_list[2], (FF, D), FF ** -0.5, 0.046875, ((0, 4), (1, 4)), jnp.float32)
    return {"out_grad": out_grad, "hidden": hidden, "weight": weight}


def reference(out_grad, hidden, weight):
    weight_grad = lax.dot_general(hidden, out_grad, (((0,), (0,)), ((), ())), precision=lax.Precision.HIGHEST, preferred_element_type=jnp.float32)
    hidden_grad = lax.dot_general(out_grad, weight, (((1,), (1,)), ((), ())), precision=lax.Precision.HIGHEST, preferred_element_type=jnp.float32)
    return weight_grad, hidden_grad
```

```python
import functools

import jax
import jax.numpy as jnp
from jax import lax
from jax.experimental import pallas as pl
from jax.experimental.pallas import tpu as pltpu
from jax.sharding import PartitionSpec as P

MESH = pl.DeviceIdType.MESH
CHUNKS = 7


def split(x):
    high = x.astype(jnp.bfloat16)
    return high, (x - high.astype(jnp.float32)).astype(jnp.bfloat16)


def exchange(
    n_row, n_col, g_ref, h_ref, w_ref, g_all, h_all, out_ref,
    w_buf, g_parts, part, from_left, from_right,
    w_sem, own_sem, gx_send, gx_recv, gs_send, gs_recv,
    ag_send, ag_recv, rs_send, rs_recv,
):
    t, ff = h_ref.shape
    tg = g_ref.shape[0]
    width = ff // CHUNKS
    tokens = n_row * tg
    chips = n_row // 2
    row, z = lax.axis_index("row"), lax.axis_index("col")
    core = lax.rem(row, 2)
    chip = row // 2
    sibling = row + 1 - 2 * core
    not_first, not_last = z > 0, z < n_col - 1

    def w_copy(c):
        rows = pl.ds(c * width, width)
        return pltpu.make_async_copy(w_ref.at[rows], w_buf.at[rows], w_sem.at[c])

    for c in range(CHUNKS):
        w_copy(c).start()
    own_h = pltpu.make_async_copy(
        h_ref, h_all.at[pl.ds(pl.multiple_of(z * t, t), t)], own_sem.at[0]
    )
    own_g = pltpu.make_async_copy(
        g_ref, g_all.at[pl.ds(pl.multiple_of(row * tg, tg), tg)], own_sem.at[1]
    )
    own_h.start()
    own_g.start()

    barrier = pltpu.get_barrier_semaphore()

    def greet(where):
        pl.semaphore_signal(barrier, inc=1, device_id=where, device_id_type=MESH)

    def peer(k):
        return lax.rem(chip + k, chips) * 2 + core

    for k in range(1, chips):
        greet({"row": peer(k)})
    greet({"row": sibling})

    @pl.when(not_first)
    def _():
        greet({"col": z - 1})

    @pl.when(not_last)
    def _():
        greet({"col": z + 1})

    pl.semaphore_wait(
        barrier, chips + not_first.astype(jnp.int32) + not_last.astype(jnp.int32)
    )

    def g_rows(r):
        return g_all.at[pl.ds(pl.multiple_of(r * tg, tg), tg)]

    def across(k):
        return pltpu.make_async_remote_copy(
            g_ref, g_rows(row), gx_send.at[k - 1], gx_recv.at[k - 1],
            device_id={"row": peer(k)}, device_id_type=MESH,
        )

    def arrived(k):
        source = lax.rem(chip + chips - k, chips) * 2 + core
        return pltpu.make_async_remote_copy(
            g_ref, g_rows(source), gx_send.at[k - 1], gx_recv.at[k - 1],
            device_id={"row": source}, device_id_type=MESH,
        )

    def aside(k, mine):
        owner = lax.rem(chip + chips - k, chips) * 2 + (core if mine else 1 - core)
        return pltpu.make_async_remote_copy(
            g_ref if k == 0 and mine else g_rows(owner), g_rows(owner),
            gs_send.at[k], gs_recv.at[k],
            device_id={"row": sibling}, device_id_type=MESH,
        )

    for k in range(1, chips):
        across(k).start()
    aside(0, True).start()

    def ag(flow, hop, c, shard):
        cols = pl.ds(pl.multiple_of(c * width, width), width)
        rows = pl.ds(pl.multiple_of(shard * t, t), t)
        source = h_ref.at[:, cols] if hop is None else h_all.at[rows, cols]
        index = c if hop is None else hop * CHUNKS + c
        return pltpu.make_async_remote_copy(
            source, h_all.at[rows, cols],
            ag_send.at[flow, index], ag_recv.at[flow, index],
            device_id={"col": z + 1 - 2 * flow}, device_id_type=MESH,
        )

    def going(flow):
        return not_first if flow else not_last

    for c in range(CHUNKS):
        for flow in range(2):

            @pl.when(going(flow))
            def _():
                ag(flow, None, c, z).start()

    def pass_on(hop, c):
        for flow in range(2):
            shard = z + hop if flow else z - hop
            there = (shard < n_col) if flow else (shard >= 0)

            @pl.when(there)
            def _():
                ag(flow, hop - 1, c, shard).wait_recv()

            @pl.when(there & going(flow))
            def _():
                ag(flow, hop, c, shard).start()

    half = CHUNKS // 2
    for c in range(half):
        pass_on(1, c)
    for k in range(1, chips):
        arrived(k).wait_recv()
        aside(k, True).start()
    for c in range(half, CHUNKS):
        pass_on(1, c)
    for k in range(chips):
        aside(k, False).wait_recv()
    own_g.wait()
    own_h.wait()
    high, low = split(g_all[...])
    g_parts[pl.ds(0, tokens)] = high
    g_parts[pl.ds(tokens, tokens)] = low

    def rs(flow, d, c):
        held = from_right if flow else from_left
        view = held.at[pl.ds(d * t, t), pl.ds(pl.multiple_of(c * width, width), width)]
        index = d * CHUNKS + c
        return pltpu.make_async_remote_copy(
            view, view, rs_send.at[flow, index], rs_recv.at[flow, index],
            device_id={"col": z + 1 - 2 * flow}, device_id_type=MESH,
        )

    def sums(flow, c):
        held = from_right if flow else from_left
        cols = pl.ds(pl.multiple_of(c * width, width), width)
        first = (z == n_col - 1) if flow else (z == 0)
        for d in range(n_col) if flow else range(n_col - 1, -1, -1):
            rows = pl.ds(d * t, t)
            on = (d < z) if flow else (d > z)

            @pl.when(jnp.logical_not(first) & (on | (z == d)))
            def _():
                rs(flow, d, c).wait_recv()

            @pl.when(on & first)
            def _():
                held[rows, cols] = part[rows, cols]

            @pl.when(on & jnp.logical_not(first))
            def _():
                held[rows, cols] += part[rows, cols]

            @pl.when(on)
            def _():
                rs(flow, d, c).start()

    contract = (((1,), (1,)), ((), ()))

    def step(i, carry):
        @pl.when(i < CHUNKS)
        def _():
            c = i
            w_copy(c).wait()
            at = pl.ds(pl.multiple_of(c * width, width), width)
            w_high, w_low = split(w_buf[at, :])
            both = lax.dot_general(
                g_parts[...], w_high, contract, preferred_element_type=jnp.float32
            )
            rest = lax.dot_general(
                g_parts[pl.ds(0, tokens)], w_low, contract,
                preferred_element_type=jnp.float32,
            )
            part[:, at] = both[:tokens] + (both[tokens:] + rest)

        for flow in range(2):
            c = i - (n_col - 1 - z if flow else z)

            @pl.when((c >= 0) & (c < CHUNKS))
            def _():
                sums(flow, c)

        @pl.when(i < (n_col - 2) * CHUNKS)
        def _():
            pass_on(i // CHUNKS + 2, lax.rem(i, CHUNKS))

        return carry

    lax.fori_loop(0, max(CHUNKS + n_col - 1, (n_col - 2) * CHUNKS), step, 0)

    mine = pl.ds(pl.multiple_of(z * t, t), t)
    out_ref[...] = part[mine]

    @pl.when(not_first)
    def _():
        out_ref[...] += from_left[mine]

    @pl.when(not_last)
    def _():
        out_ref[...] += from_right[mine]

    for k in range(1, chips):
        across(k).wait_send()
    for k in range(chips):
        aside(k, True).wait_send()

    def drain(c, carry):
        for flow in range(2):

            @pl.when(going(flow))
            def _():
                ag(flow, None, c, z).wait_send()

            for hop in range(1, n_col - 1):
                shard = z + hop if flow else z - hop
                there = (shard < n_col) if flow else (shard >= 0)

                @pl.when(there & going(flow))
                def _():
                    ag(flow, hop, c, shard).wait_send()

            for d in range(n_col):

                @pl.when((d < z) if flow else (d > z))
                def _():
                    rs(flow, d, c).wait_send()

        return carry

    lax.fori_loop(0, CHUNKS, drain, 0)


def outer(tile, h_ref, g_ref, out_ref, g_parts):
    tokens = g_ref.shape[0]

    @pl.when(pl.program_id(0) == 0)
    def _():
        high, low = split(g_ref[...])
        g_parts[pl.ds(0, tokens)] = high
        g_parts[pl.ds(tokens, tokens)] = low
        g_parts[pl.ds(2 * tokens, tokens)] = high

    at = pl.ds(pl.multiple_of(pl.program_id(0) * tile, tile), tile)
    high, low = split(h_ref[:, at])
    out_ref[...] = lax.dot_general(
        jnp.concatenate([high, high, low], axis=0), g_parts[...],
        (((0,), (0,)), ((), ())), preferred_element_type=jnp.float32,
    )


def on_device(n_row, n_col, out_grad, hidden, weight):
    f32 = jnp.float32
    (tg, d), (t, ff) = out_grad.shape, hidden.shape
    tokens = n_row * tg
    dma = pltpu.SemaphoreType.DMA
    whole = pl.BlockSpec(memory_space=pltpu.VMEM)
    chips = n_row // 2
    g_all, h_all, hidden_grad = pl.pallas_call(
        functools.partial(exchange, n_row, n_col),
        out_shape=(
            jax.ShapeDtypeStruct((tokens, d), f32),
            jax.ShapeDtypeStruct((tokens, ff), f32),
            jax.ShapeDtypeStruct((t, ff), f32),
        ),
        in_specs=[pl.BlockSpec(memory_space=pl.ANY)] * 3,
        out_specs=(whole,) * 3,
        scratch_shapes=[
            pltpu.VMEM((ff, d), f32),
            pltpu.VMEM((2 * tokens, d), jnp.bfloat16),
            pltpu.VMEM((tokens, ff), f32),
            pltpu.VMEM((tokens, ff), f32),
            pltpu.VMEM((tokens, ff), f32),
            dma((CHUNKS,)),
            dma((2,)),
            dma((max(chips - 1, 1),)),
            dma((max(chips - 1, 1),)),
            dma((chips,)),
            dma((chips,)),
            dma((2, (n_col - 1) * CHUNKS)),
            dma((2, (n_col - 1) * CHUNKS)),
            dma((2, n_col * CHUNKS)),
            dma((2, n_col * CHUNKS)),
        ],
        compiler_params=pltpu.CompilerParams(
            collective_id=0, has_side_effects=True, vmem_limit_bytes=56 << 20
        ),
        name="exchange",
    )(out_grad, hidden, weight)
    tile = 256 if ff % 256 == 0 and ff > 1024 else 128
    weight_grad = pl.pallas_call(
        functools.partial(outer, tile),
        grid=(ff // tile,),
        out_shape=jax.ShapeDtypeStruct((ff, d), f32),
        in_specs=[whole, whole],
        out_specs=pl.BlockSpec((tile, d), lambda i: (i, 0)),
        scratch_shapes=[pltpu.VMEM((3 * tokens, d), jnp.bfloat16)],
        compiler_params=pltpu.CompilerParams(vmem_limit_bytes=40 << 20),
        name="outer",
    )(h_all, g_all)
    return (weight_grad, hidden_grad)


def solution(mesh):
    placed = (P(("dp", "row"), "col"), P(("dp", "col"), "row"), P("row", "col"))
    return jax.shard_map(
        functools.partial(on_device, mesh.shape["row"], mesh.shape["col"]),
        mesh=mesh,
        in_specs=placed,
        out_specs=(P(("dp", "row"), "col"), P(("dp", "col"), "row")),
        check_vma=False,
    )
```

```python
import functools

import jax
import jax.numpy as jnp
from jax import lax
from jax.experimental import pallas as pl
from jax.experimental.pallas import tpu as pltpu
from jax.sharding import PartitionSpec as P

MESH = pl.DeviceIdType.MESH
CHUNKS = 7
LAG = 2
PASSES = 2


def split(x):
    high = x.astype(jnp.bfloat16)
    return high, (x - high.astype(jnp.float32)).astype(jnp.bfloat16)


def exchange(
    n_row, n_col, g_ref, h_ref, w_ref, g_out, h_out, out_ref,
    g_all, h_all, w_buf, g_parts, part, from_left, from_right,
    w_sem, own_sem, gx_send, gx_recv, gs_send, gs_recv,
    ag_send, ag_recv, rs_send, rs_recv,
):
    t, ff = h_ref.shape
    tg = g_ref.shape[0]
    width = ff // CHUNKS
    tokens = n_row * tg
    chips = n_row // 2
    row, z = lax.axis_index("row"), lax.axis_index("col")
    core = lax.rem(row, 2)
    chip = row // 2
    sibling = row + 1 - 2 * core
    not_first, not_last = z > 0, z < n_col - 1

    def w_copy(c):
        rows = pl.ds(c * width, width)
        return pltpu.make_async_copy(w_ref.at[rows], w_buf.at[rows], w_sem.at[c])

    for c in range(CHUNKS):
        w_copy(c).start()
    own_h = pltpu.make_async_copy(
        h_ref, h_all.at[pl.ds(pl.multiple_of(z * t, t), t)], own_sem.at[0]
    )
    own_g = pltpu.make_async_copy(
        g_ref, g_all.at[pl.ds(pl.multiple_of(row * tg, tg), tg)], own_sem.at[1]
    )
    own_h.start()
    own_g.start()

    barrier = pltpu.get_barrier_semaphore()

    def greet(where):
        pl.semaphore_signal(barrier, inc=1, device_id=where, device_id_type=MESH)

    def peer(k):
        return lax.rem(chip + k, chips) * 2 + core

    for k in range(1, chips):
        greet({"row": peer(k)})
    greet({"row": sibling})

    @pl.when(not_first)
    def _():
        greet({"col": z - 1})

    @pl.when(not_last)
    def _():
        greet({"col": z + 1})

    pl.semaphore_wait(
        barrier, chips + not_first.astype(jnp.int32) + not_last.astype(jnp.int32)
    )

    def g_rows(r):
        return g_all.at[pl.ds(pl.multiple_of(r * tg, tg), tg)]

    def across(k):
        return pltpu.make_async_remote_copy(
            g_ref, g_rows(row), gx_send.at[k - 1], gx_recv.at[k - 1],
            device_id={"row": peer(k)}, device_id_type=MESH,
        )

    def arrived(k):
        source = lax.rem(chip + chips - k, chips) * 2 + core
        return pltpu.make_async_remote_copy(
            g_ref, g_rows(source), gx_send.at[k - 1], gx_recv.at[k - 1],
            device_id={"row": source}, device_id_type=MESH,
        )

    def aside(k, mine):
        owner = lax.rem(chip + chips - k, chips) * 2 + (core if mine else 1 - core)
        return pltpu.make_async_remote_copy(
            g_ref if k == 0 and mine else g_rows(owner), g_rows(owner),
            gs_send.at[k], gs_recv.at[k],
            device_id={"row": sibling}, device_id_type=MESH,
        )

    for k in range(1, chips):
        across(k).start()
    aside(0, True).start()

    def ag(flow, hop, c, shard):
        cols = pl.ds(pl.multiple_of(c * width, width), width)
        rows = pl.ds(pl.multiple_of(shard * t, t), t)
        source = h_ref.at[:, cols] if hop is None else h_all.at[rows, cols]
        index = c if hop is None else hop * CHUNKS + c
        return pltpu.make_async_remote_copy(
            source, h_all.at[rows, cols],
            ag_send.at[flow, index], ag_recv.at[flow, index],
            device_id={"col": z + 1 - 2 * flow}, device_id_type=MESH,
        )

    def going(flow):
        return not_first if flow else not_last

    for c in range(CHUNKS):
        for flow in range(2):

            @pl.when(going(flow))
            def _():
                ag(flow, None, c, z).start()

    def pass_on(hop, c):
        for flow in range(2):
            shard = z + hop if flow else z - hop
            there = (shard < n_col) if flow else (shard >= 0)

            @pl.when(there)
            def _():
                ag(flow, hop - 1, c, shard).wait_recv()

            @pl.when(there & going(flow))
            def _():
                ag(flow, hop, c, shard).start()

    half = CHUNKS // 2
    for c in range(half):
        pass_on(1, c)
    for k in range(1, chips):
        arrived(k).wait_recv()
        aside(k, True).start()
    for c in range(half, CHUNKS):
        pass_on(1, c)
    for k in range(chips):
        aside(k, False).wait_recv()
    own_g.wait()
    own_h.wait()
    high, low = split(g_all[...])
    g_parts[pl.ds(0, tokens)] = high
    g_parts[pl.ds(tokens, tokens)] = low
    give_g = pltpu.make_async_copy(g_all, g_out, own_sem.at[0])
    give_h = pltpu.make_async_copy(h_all, h_out, own_sem.at[1])
    give_g.start()

    def rs(flow, d, c):
        held = from_right if flow else from_left
        view = held.at[pl.ds(d * t, t), pl.ds(pl.multiple_of(c * width, width), width)]
        index = d * CHUNKS + c
        return pltpu.make_async_remote_copy(
            view, view, rs_send.at[flow, index], rs_recv.at[flow, index],
            device_id={"col": z + 1 - 2 * flow}, device_id_type=MESH,
        )

    def sums(flow, c):
        held = from_right if flow else from_left
        cols = pl.ds(pl.multiple_of(c * width, width), width)
        first = (z == n_col - 1) if flow else (z == 0)
        for d in range(n_col) if flow else range(n_col - 1, -1, -1):
            rows = pl.ds(d * t, t)
            on = (d < z) if flow else (d > z)

            @pl.when(jnp.logical_not(first) & (on | (z == d)))
            def _():
                rs(flow, d, c).wait_recv()

            @pl.when(on & first)
            def _():
                held[rows, cols] = part[rows, cols]

            @pl.when(on & jnp.logical_not(first))
            def _():
                held[rows, cols] += part[rows, cols]

            @pl.when(on)
            def _():
                rs(flow, d, c).start()

    contract = (((1,), (1,)), ((), ()))

    items = (n_col - 2) * CHUNKS
    passes = -(-items // PASSES)

    def step(i, carry):
        @pl.when(i < CHUNKS)
        def _():
            c = i
            w_copy(c).wait()
            at = pl.ds(pl.multiple_of(c * width, width), width)
            w_high, w_low = split(w_buf[at, :])
            both = lax.dot_general(
                g_parts[...], w_high, contract, preferred_element_type=jnp.float32
            )
            rest = lax.dot_general(
                g_parts[pl.ds(0, tokens)], w_low, contract,
                preferred_element_type=jnp.float32,
            )
            part[:, at] = both[:tokens] + (both[tokens:] + rest)

        for k in range(PASSES):
            item = PASSES * i + k

            @pl.when(item < items)
            def _():
                pass_on(item // CHUNKS + 2, lax.rem(item, CHUNKS))

        @pl.when(i == passes - 1)
        def _():
            give_h.start()

        for flow in range(2):
            c = i - LAG * (n_col - 1 - z if flow else z)

            @pl.when((c >= 0) & (c < CHUNKS))
            def _():
                sums(flow, c)

        return carry

    lax.fori_loop(0, max(CHUNKS + LAG * (n_col - 1), passes), step, 0)

    mine = pl.ds(pl.multiple_of(z * t, t), t)
    out_ref[...] = part[mine]

    @pl.when(not_first)
    def _():
        out_ref[...] += from_left[mine]

    @pl.when(not_last)
    def _():
        out_ref[...] += from_right[mine]

    for k in range(1, chips):
        across(k).wait_send()
    for k in range(chips):
        aside(k, True).wait_send()

    def drain(c, carry):
        for flow in range(2):

            @pl.when(going(flow))
            def _():
                ag(flow, None, c, z).wait_send()

            for hop in range(1, n_col - 1):
                shard = z + hop if flow else z - hop
                there = (shard < n_col) if flow else (shard >= 0)

                @pl.when(there & going(flow))
                def _():
                    ag(flow, hop, c, shard).wait_send()

            for d in range(n_col):

                @pl.when((d < z) if flow else (d > z))
                def _():
                    rs(flow, d, c).wait_send()

        return carry

    lax.fori_loop(0, CHUNKS, drain, 0)
    give_g.wait()
    give_h.wait()


def outer(
    tile, h_ref, g_ref, hg_ref, out_ref, hg_out,
    h_buf, g_buf, g_parts, buf, in_sem, out_sem,
):
    tokens, ff = h_ref.shape
    width = ff // CHUNKS
    moved = pltpu.make_async_copy(hg_ref, hg_out, in_sem.at[CHUNKS + 1])
    g_in = pltpu.make_async_copy(g_ref, g_buf, in_sem.at[CHUNKS])
    g_in.start()

    def h_in(c):
        at = pl.ds(c * width, width)
        return pltpu.make_async_copy(h_ref.at[:, at], h_buf.at[:, at], in_sem.at[c])

    for c in range(CHUNKS):
        h_in(c).start()
    moved.start()
    g_in.wait()
    high, low = split(g_buf[...])
    g_parts[pl.ds(0, tokens)] = high
    g_parts[pl.ds(tokens, tokens)] = low
    g_parts[pl.ds(2 * tokens, tokens)] = high

    def give(i):
        at = pl.ds(i * tile, tile)
        return pltpu.make_async_copy(buf.at[at], out_ref.at[at], out_sem.at[i])

    for i in range(ff // tile):
        if i * tile % width == 0:
            h_in(i * tile // width).wait()
        at = pl.ds(i * tile, tile)
        high, low = split(h_buf[:, at])
        buf[at] = lax.dot_general(
            jnp.concatenate([high, high, low], axis=0), g_parts[...],
            (((0,), (0,)), ((), ())), preferred_element_type=jnp.float32,
        )
        give(i).start()
    for i in range(ff // tile):
        give(i).wait()
    moved.wait()


def on_device(n_row, n_col, out_grad, hidden, weight):
    f32 = jnp.float32
    (tg, d), (t, ff) = out_grad.shape, hidden.shape
    tokens = n_row * tg
    dma = pltpu.SemaphoreType.DMA
    whole = pl.BlockSpec(memory_space=pltpu.VMEM)
    anywhere = pl.BlockSpec(memory_space=pltpu.HBM)
    chips = n_row // 2
    g_all, h_all, hidden_grad = pl.pallas_call(
        functools.partial(exchange, n_row, n_col),
        out_shape=(
            jax.ShapeDtypeStruct((tokens, d), f32),
            jax.ShapeDtypeStruct((tokens, ff), f32),
            jax.ShapeDtypeStruct((t, ff), f32),
        ),
        in_specs=[anywhere] * 3,
        out_specs=(anywhere, anywhere, whole),
        scratch_shapes=[
            pltpu.VMEM((tokens, d), f32),
            pltpu.VMEM((tokens, ff), f32),
            pltpu.VMEM((ff, d), f32),
            pltpu.VMEM((2 * tokens, d), jnp.bfloat16),
            pltpu.VMEM((tokens, ff), f32),
            pltpu.VMEM((tokens, ff), f32),
            pltpu.VMEM((tokens, ff), f32),
            dma((CHUNKS,)),
            dma((2,)),
            dma((max(chips - 1, 1),)),
            dma((max(chips - 1, 1),)),
            dma((chips,)),
            dma((chips,)),
            dma((2, (n_col - 1) * CHUNKS)),
            dma((2, (n_col - 1) * CHUNKS)),
            dma((2, n_col * CHUNKS)),
            dma((2, n_col * CHUNKS)),
        ],
        compiler_params=pltpu.CompilerParams(
            collective_id=0, has_side_effects=True, vmem_limit_bytes=56 << 20
        ),
        name="exchange",
    )(out_grad, hidden, weight)
    tile = 256 if ff % 256 == 0 and ff > 1024 else 128
    weight_grad, hidden_grad = pl.pallas_call(
        functools.partial(outer, tile),
        out_shape=(
            jax.ShapeDtypeStruct((ff, d), f32),
            jax.ShapeDtypeStruct((t, ff), f32),
        ),
        in_specs=[anywhere] * 3,
        out_specs=(anywhere,) * 2,
        scratch_shapes=[
            pltpu.VMEM((tokens, ff), f32),
            pltpu.VMEM((tokens, d), f32),
            pltpu.VMEM((3 * tokens, d), jnp.bfloat16),
            pltpu.VMEM((ff, d), f32),
            dma((CHUNKS + 2,)),
            dma((ff // tile,)),
        ],
        compiler_params=pltpu.CompilerParams(vmem_limit_bytes=56 << 20),
        name="outer",
    )(h_all, g_all, hidden_grad)
    return (weight_grad, hidden_grad)


def solution(mesh):
    placed = (P(("dp", "row"), "col"), P(("dp", "col"), "row"), P("row", "col"))
    return jax.shard_map(
        functools.partial(on_device, mesh.shape["row"], mesh.shape["col"]),
        mesh=mesh,
        in_specs=placed,
        out_specs=(P(("dp", "row"), "col"), P(("dp", "col"), "row")),
        check_vma=False,
    )
```

```python
import functools

import jax
import jax.numpy as jnp
from jax import lax
from jax.experimental import pallas as pl
from jax.experimental.pallas import tpu as pltpu
from jax.sharding import PartitionSpec as P

MESH = pl.DeviceIdType.MESH
CHUNKS = 7
LAG = 2
PASSES = 2


def split(x):
    high = x.astype(jnp.bfloat16)
    return high, (x - high.astype(jnp.float32)).astype(jnp.bfloat16)


def exchange(
    n_row, n_col, g_ref, h_ref, w_ref, g_out, h_out, out_ref,
    g_all, h_all, w_buf, g_parts, part, from_left, from_right, near,
    w_sem, own_sem, gx_send, gx_recv, gs_send, gs_recv,
    ag_send, ag_recv, rs_send, rs_recv, near_send, near_recv,
):
    t, ff = h_ref.shape
    tg = g_ref.shape[0]
    width = ff // CHUNKS
    tokens = n_row * tg
    chips = n_row // 2
    row, z = lax.axis_index("row"), lax.axis_index("col")
    core = lax.rem(row, 2)
    chip = row // 2
    sibling = row + 1 - 2 * core
    not_first, not_last = z > 0, z < n_col - 1

    def w_copy(c):
        rows = pl.ds(c * width, width)
        return pltpu.make_async_copy(w_ref.at[rows], w_buf.at[rows], w_sem.at[c])

    for c in range(CHUNKS):
        w_copy(c).start()
    own_h = pltpu.make_async_copy(
        h_ref, h_all.at[pl.ds(pl.multiple_of(z * t, t), t)], own_sem.at[0]
    )
    own_g = pltpu.make_async_copy(
        g_ref, g_all.at[pl.ds(pl.multiple_of(row * tg, tg), tg)], own_sem.at[1]
    )
    own_h.start()
    own_g.start()

    barrier = pltpu.get_barrier_semaphore()

    def greet(where):
        pl.semaphore_signal(barrier, inc=1, device_id=where, device_id_type=MESH)

    def peer(k):
        return lax.rem(chip + k, chips) * 2 + core

    for k in range(1, chips):
        greet({"row": peer(k)})
    greet({"row": sibling})

    for k in range(1, n_col):
        greet({"col": lax.rem(z + k, n_col)})
    pl.semaphore_wait(barrier, chips + n_col - 1)

    def g_rows(r):
        return g_all.at[pl.ds(pl.multiple_of(r * tg, tg), tg)]

    def across(k):
        return pltpu.make_async_remote_copy(
            g_ref, g_rows(row), gx_send.at[k - 1], gx_recv.at[k - 1],
            device_id={"row": peer(k)}, device_id_type=MESH,
        )

    def arrived(k):
        source = lax.rem(chip + chips - k, chips) * 2 + core
        return pltpu.make_async_remote_copy(
            g_ref, g_rows(source), gx_send.at[k - 1], gx_recv.at[k - 1],
            device_id={"row": source}, device_id_type=MESH,
        )

    def aside(k, mine):
        owner = lax.rem(chip + chips - k, chips) * 2 + (core if mine else 1 - core)
        return pltpu.make_async_remote_copy(
            g_ref if k == 0 and mine else g_rows(owner), g_rows(owner),
            gs_send.at[k], gs_recv.at[k],
            device_id={"row": sibling}, device_id_type=MESH,
        )

    for k in range(1, chips):
        across(k).start()
    aside(0, True).start()

    def ag(flow, hop, c, shard):
        cols = pl.ds(pl.multiple_of(c * width, width), width)
        rows = pl.ds(pl.multiple_of(shard * t, t), t)
        source = h_ref.at[:, cols] if hop is None else h_all.at[rows, cols]
        index = c if hop is None else hop * CHUNKS + c
        return pltpu.make_async_remote_copy(
            source, h_all.at[rows, cols],
            ag_send.at[flow, index], ag_recv.at[flow, index],
            device_id={"col": z + 1 - 2 * flow}, device_id_type=MESH,
        )

    def going(flow):
        return not_first if flow else not_last

    for c in range(CHUNKS):
        for flow in range(2):

            @pl.when(going(flow))
            def _():
                ag(flow, None, c, z).start()

    def pass_on(hop, c):
        for flow in range(2):
            shard = z + hop if flow else z - hop
            there = (shard < n_col) if flow else (shard >= 0)

            @pl.when(there)
            def _():
                ag(flow, hop - 1, c, shard).wait_recv()

            @pl.when(there & going(flow))
            def _():
                ag(flow, hop, c, shard).start()

    half = CHUNKS // 2
    for c in range(half):
        pass_on(1, c)
    for k in range(1, chips):
        arrived(k).wait_recv()
        aside(k, True).start()
    for c in range(half, CHUNKS):
        pass_on(1, c)
    for k in range(chips):
        aside(k, False).wait_recv()
    own_g.wait()
    own_h.wait()
    high, low = split(g_all[...])
    g_parts[pl.ds(0, tokens)] = high
    g_parts[pl.ds(tokens, tokens)] = low
    give_g = pltpu.make_async_copy(g_all, g_out, own_sem.at[0])
    give_h = pltpu.make_async_copy(h_all, h_out, own_sem.at[1])
    give_g.start()

    def rs(flow, d, c):
        held = from_right if flow else from_left
        view = held.at[pl.ds(d * t, t), pl.ds(pl.multiple_of(c * width, width), width)]
        index = d * CHUNKS + c
        return pltpu.make_async_remote_copy(
            view, view, rs_send.at[flow, index], rs_recv.at[flow, index],
            device_id={"col": z + 1 - 2 * flow}, device_id_type=MESH,
        )

    def sums(flow, c):
        held = from_right if flow else from_left
        cols = pl.ds(pl.multiple_of(c * width, width), width)
        first = (z == n_col - 1) if flow else (z == 0)
        for d in range(n_col) if flow else range(n_col - 1, -1, -1):
            rows = pl.ds(d * t, t)
            on = (d < z) if flow else (d > z)

            @pl.when(jnp.logical_not(first) & (on | (z == d)))
            def _():
                rs(flow, d, c).wait_recv()

            @pl.when(on & first)
            def _():
                held[rows, cols] = part[rows, cols]

            @pl.when(on & jnp.logical_not(first))
            def _():
                held[rows, cols] += part[rows, cols]

            @pl.when(on)
            def _():
                rs(flow, d, c).start()

    last = (CHUNKS - 1) * width

    def straight(k):
        owner = lax.rem(z + k, n_col)
        rows = pl.ds(pl.multiple_of(owner * t, t), t)
        return pltpu.make_async_remote_copy(
            part.at[rows, pl.ds(last, width)], near.at[k - 1],
            near_send.at[k - 1], near_recv.at[k - 1],
            device_id={"col": owner}, device_id_type=MESH,
        )

    contract = (((1,), (1,)), ((), ()))

    items = (n_col - 2) * CHUNKS
    passes = -(-items // PASSES)

    def step(i, carry):
        @pl.when(i < CHUNKS)
        def _():
            c = i
            w_copy(c).wait()
            at = pl.ds(pl.multiple_of(c * width, width), width)
            w_high, w_low = split(w_buf[at, :])
            both = lax.dot_general(
                g_parts[...], w_high, contract, preferred_element_type=jnp.float32
            )
            rest = lax.dot_general(
                g_parts[pl.ds(0, tokens)], w_low, contract,
                preferred_element_type=jnp.float32,
            )
            part[:, at] = both[:tokens] + (both[tokens:] + rest)

        @pl.when(i == CHUNKS - 1)
        def _():
            for k in range(1, n_col):
                straight(k).start()

        for k in range(PASSES):
            item = PASSES * i + k

            @pl.when(item < items)
            def _():
                pass_on(item // CHUNKS + 2, lax.rem(item, CHUNKS))

        @pl.when(i == passes - 1)
        def _():
            give_h.start()

        for flow in range(2):
            c = i - LAG * (n_col - 1 - z if flow else z)

            @pl.when((c >= 0) & (c < CHUNKS - 1))
            def _():
                sums(flow, c)

        return carry

    lax.fori_loop(0, max(CHUNKS + LAG * (n_col - 1), passes), step, 0)

    mine = pl.ds(pl.multiple_of(z * t, t), t)
    out_ref[...] = part[mine]

    @pl.when(not_first)
    def _():
        out_ref[:, pl.ds(0, last)] += from_left[mine, pl.ds(0, last)]

    @pl.when(not_last)
    def _():
        out_ref[:, pl.ds(0, last)] += from_right[mine, pl.ds(0, last)]

    for k in range(1, n_col):
        straight(k).wait_recv()
        out_ref[:, pl.ds(last, width)] += near[k - 1]
    for k in range(1, n_col):
        straight(k).wait_send()

    for k in range(1, chips):
        across(k).wait_send()
    for k in range(chips):
        aside(k, True).wait_send()

    def drain(c, carry):
        for flow in range(2):

            @pl.when(going(flow))
            def _():
                ag(flow, None, c, z).wait_send()

            for hop in range(1, n_col - 1):
                shard = z + hop if flow else z - hop
                there = (shard < n_col) if flow else (shard >= 0)

                @pl.when(there & going(flow))
                def _():
                    ag(flow, hop, c, shard).wait_send()

            for d in range(n_col):

                @pl.when((c < CHUNKS - 1) & ((d < z) if flow else (d > z)))
                def _():
                    rs(flow, d, c).wait_send()

        return carry

    lax.fori_loop(0, CHUNKS, drain, 0)
    give_g.wait()
    give_h.wait()


def outer(
    tile, h_ref, g_ref, hg_ref, out_ref, hg_out,
    h_buf, g_buf, g_parts, buf, in_sem, out_sem,
):
    tokens, ff = h_ref.shape
    width = ff // CHUNKS
    moved = pltpu.make_async_copy(hg_ref, hg_out, in_sem.at[CHUNKS + 1])
    g_in = pltpu.make_async_copy(g_ref, g_buf, in_sem.at[CHUNKS])
    g_in.start()

    def h_in(c):
        at = pl.ds(c * width, width)
        return pltpu.make_async_copy(h_ref.at[:, at], h_buf.at[:, at], in_sem.at[c])

    for c in range(CHUNKS):
        h_in(c).start()
    moved.start()
    g_in.wait()
    high, low = split(g_buf[...])
    g_parts[pl.ds(0, tokens)] = high
    g_parts[pl.ds(tokens, tokens)] = low
    g_parts[pl.ds(2 * tokens, tokens)] = high

    def give(i):
        at = pl.ds(i * tile, tile)
        return pltpu.make_async_copy(buf.at[at], out_ref.at[at], out_sem.at[i])

    for i in range(ff // tile):
        if i * tile % width == 0:
            h_in(i * tile // width).wait()
        at = pl.ds(i * tile, tile)
        high, low = split(h_buf[:, at])
        buf[at] = lax.dot_general(
            jnp.concatenate([high, high, low], axis=0), g_parts[...],
            (((0,), (0,)), ((), ())), preferred_element_type=jnp.float32,
        )
        give(i).start()
    for i in range(ff // tile):
        give(i).wait()
    moved.wait()


def on_device(n_row, n_col, out_grad, hidden, weight):
    f32 = jnp.float32
    (tg, d), (t, ff) = out_grad.shape, hidden.shape
    tokens = n_row * tg
    dma = pltpu.SemaphoreType.DMA
    whole = pl.BlockSpec(memory_space=pltpu.VMEM)
    anywhere = pl.BlockSpec(memory_space=pltpu.HBM)
    chips = n_row // 2
    g_all, h_all, hidden_grad = pl.pallas_call(
        functools.partial(exchange, n_row, n_col),
        out_shape=(
            jax.ShapeDtypeStruct((tokens, d), f32),
            jax.ShapeDtypeStruct((tokens, ff), f32),
            jax.ShapeDtypeStruct((t, ff), f32),
        ),
        in_specs=[anywhere] * 3,
        out_specs=(anywhere, anywhere, whole),
        scratch_shapes=[
            pltpu.VMEM((tokens, d), f32),
            pltpu.VMEM((tokens, ff), f32),
            pltpu.VMEM((ff, d), f32),
            pltpu.VMEM((2 * tokens, d), jnp.bfloat16),
            pltpu.VMEM((tokens, ff), f32),
            pltpu.VMEM((tokens, ff), f32),
            pltpu.VMEM((tokens, ff), f32),
            pltpu.VMEM((n_col - 1, t, ff // CHUNKS), f32),
            dma((CHUNKS,)),
            dma((2,)),
            dma((max(chips - 1, 1),)),
            dma((max(chips - 1, 1),)),
            dma((chips,)),
            dma((chips,)),
            dma((2, (n_col - 1) * CHUNKS)),
            dma((2, (n_col - 1) * CHUNKS)),
            dma((2, n_col * CHUNKS)),
            dma((2, n_col * CHUNKS)),
            dma((n_col - 1,)),
            dma((n_col - 1,)),
        ],
        compiler_params=pltpu.CompilerParams(
            collective_id=0, has_side_effects=True, vmem_limit_bytes=56 << 20
        ),
        name="exchange",
    )(out_grad, hidden, weight)
    tile = 256 if ff % 256 == 0 and ff > 1024 else 128
    weight_grad, hidden_grad = pl.pallas_call(
        functools.partial(outer, tile),
        out_shape=(
            jax.ShapeDtypeStruct((ff, d), f32),
            jax.ShapeDtypeStruct((t, ff), f32),
        ),
        in_specs=[anywhere] * 3,
        out_specs=(anywhere,) * 2,
        scratch_shapes=[
            pltpu.VMEM((tokens, ff), f32),
            pltpu.VMEM((tokens, d), f32),
            pltpu.VMEM((3 * tokens, d), jnp.bfloat16),
            pltpu.VMEM((ff, d), f32),
            dma((CHUNKS + 2,)),
            dma((ff // tile,)),
        ],
        compiler_params=pltpu.CompilerParams(vmem_limit_bytes=56 << 20),
        name="outer",
    )(h_all, g_all, hidden_grad)
    return (weight_grad, hidden_grad)


def solution(mesh):
    placed = (P(("dp", "row"), "col"), P(("dp", "col"), "row"), P("row", "col"))
    return jax.shard_map(
        functools.partial(on_device, mesh.shape["row"], mesh.shape["col"]),
        mesh=mesh,
        in_specs=placed,
        out_specs=(P(("dp", "row"), "col"), P(("dp", "col"), "row")),
        check_vma=False,
    )
```
